256 devices in a mesh: row: 16 (over x_lo, y, core), col: 16 (over x_hi, z).
Axes of the slice: x: 4 (x_hi: 2, x_lo: 2; x = x_hi * 2 + x_lo), y: 4, z: 8, core: 2. Of those that a mesh axis runs over, the one named last changes fastest.
Arguments:
- velocity: float32 [32, 768, 4096], P('col', 'row'), may hold values from -6 to 6
- stream_ops: float32 [2, 3, 128, 128], replicated, may hold values from -0.3125 to 0.3125
- normal_ops: float32 [2, 768, 768], replicated, may hold values from -0.21875 to 0.21875
- span_ops: float32 [2, 32, 32], replicated, may hold values from -1 to 1
Outputs:
- grad_stream: float32 [32, 768, 4096], P(None, ('row', 'col'))
- grad_normal: float32 [32, 768, 4096], P(None, ('row', 'col'))
- grad_span: float32 [32, 768, 4096], P(None, ('row', 'col'))
The draws below stay inside these ranges and needn't reach their ends.
All inputs are finite; a program needn't handle non-finite values.
Results may differ from the reference program's by a relative error of at most 0.00007.
Values sent between devices are 32-bit elements; how exact they have to be, the bound alone decides.
No kernel may reach another device: no remote copies, remote signals or barrier semaphores. Data moves between devices by JAX's collectives and lax.ppermute only.
A program may use at most 64 MiB of HBM per device.

```python
import jax
import jax.numpy as jnp
from jax import lax

NX = 4096
NY = 768
NZ = 32
BX = 128


def block_scale(own_key, shape, split, least, top_value):
    factor_of = 1.0
    for axis_at, shards_of in split:
        draws = jax.random.uniform(jax.random.fold_in(jax.random.fold_in(own_key, 6), axis_at), (shards_of,), jnp.float32, least / len(split), top_value / len(split))
        factor_of = factor_of * jnp.repeat(jnp.exp(draws), shape[axis_at] // shards_of).reshape((-1,) + (1,) * (len(shape) - 1 - axis_at))
    return factor_of


def noise(stream_key, shape, deviation, most, split=(), kind=jnp.bfloat16):
    array = jax.random.normal(stream_key, shape, jnp.float32) * deviation
    if len(split) > 0:
        array = block_scale(stream_key, shape, split, -0.22, 0.18) * array
    return jnp.clip(array, min=-most, max=most).astype(kind)


def setup_inputs(seed: int = 0) -> dict:
    key_list = jax.random.split(jax.random.key(seed), 5)
    return {
        "velocity": noise(key_list[0], (NZ, NY, NX), 1.0, 6.0, ((0, 16), (1, 16)), jnp.float32),
        "stream_ops": noise(key_list[1], (2, 3, BX, BX), (3 * BX) ** -0.5, 0.3125, (), jnp.float32),
        "normal_ops": noise(key_list[2], (2, NY, NY), NY ** -0.5, 0.21875, (), jnp.float32),
        "span_ops": noise(key_list[3], (2, NZ, NZ), NZ ** -0.5, 1.0, (), jnp.float32),
    }


def apply_streamwise(field, stream_ops, which):
    lead = field.shape[:-1]
    blocks = field.reshape(lead + (NX // BX, BX))
    earlier = jnp.roll(blocks, 1, axis=-2)
    later = jnp.roll(blocks, -1, axis=-2)
    hp = lax.Precision.HIGHEST
    result = jnp.einsum("...bi,oi->...bo", earlier, stream_ops[which, 0], precision=hp)
    result = result + jnp.einsum("...bi,oi->...bo", blocks, stream_ops[which, 1], precision=hp)
    result = result + jnp.einsum("...bi,oi->...bo", later, stream_ops[which, 2], precision=hp)
    return result.reshape(lead + (NX,))


def apply_normal(field, matrix):
    return jnp.einsum("yk,zkx->zyx", matrix, field, precision=lax.Precision.HIGHEST)


def apply_spanwise(field, matrix):
    return jnp.einsum("zk,kyx->zyx", matrix, field, precision=lax.Precision.HIGHEST)


def reference(velocity, stream_ops, normal_ops, span_ops):
    normal_interp = apply_normal(velocity, normal_ops[0])
    normal_deriv = apply_normal(velocity, normal_ops[1])
    grad_stream = apply_spanwise(apply_streamwise(normal_interp, stream_ops, 1), span_ops[0])
    grad_normal = apply_spanwise(apply_streamwise(normal_deriv, stream_ops, 0), span_ops[0])
    grad_span = apply_spanwise(apply_streamwise(normal_interp, stream_ops, 0), span_ops[1])
    return grad_stream, grad_normal, grad_span
```

```python
import jax
import jax.numpy as jnp
from jax import lax
from jax.experimental import pallas as pl
from jax.experimental.pallas import tpu as pltpu
from jax.sharding import PartitionSpec as P

F32 = jnp.float32
BF16 = jnp.bfloat16


def split(x):
    hi = x.astype(BF16)
    return hi, (x - hi.astype(F32)).astype(BF16)


def dot(a, b):
    return jnp.dot(a, b, preferred_element_type=F32)


def params(mib):
    return pltpu.CompilerParams(vmem_limit_bytes=mib << 20)


def pack_kernel(v_ref, o_ref):
    for d in range(o_ref.shape[0]):
        for q in range(4):
            z, h = q // 2, q % 2
            o_ref[d, 48 * q : 48 * q + 48, :] = v_ref[z, :, 256 * d + 128 * h : 256 * d + 128 * h + 128]


def pack(velocity):
    steps = 4
    return pl.pallas_call(
        pack_kernel,
        out_shape=jax.ShapeDtypeStruct((16, 192, 128), F32),
        grid=(steps,),
        in_specs=[pl.BlockSpec((2, 48, 4096 // steps), lambda i: (0, 0, i))],
        out_specs=pl.BlockSpec((16 // steps, 192, 128), lambda i: (i, 0, 0)),
        compiler_params=params(16),
        cost_estimate=pl.CostEstimate(flops=0, bytes_accessed=3 << 20, transcendentals=0),
        name="pack",
    )(velocity)


def operators_kernel(n_ref, s_ref, p_ref, whi_ref, wlo_ref, bhi_ref, blo_ref, z_ref):
    for j in range(3):
        whi_ref[j, 0], wlo_ref[j, 0] = split(n_ref[0, pl.ds(j, 256, stride=3), :])

    @pl.when((pl.program_id(0) == 0) & (pl.program_id(1) == 0))
    def _():
        zero = jnp.zeros((128, 128), BF16)
        for op in range(2):
            parts = [split(s_ref[op, d].T) for d in range(3)]
            for k in range(4):
                for h in range(2):
                    inside = 0 <= k - h <= 2
                    rows, lanes = slice(128 * k, 128 * k + 128), slice(128 * h, 128 * h + 128)
                    bhi_ref[op, rows, lanes] = parts[k - h][0] if inside else zero
                    blo_ref[op, rows, lanes] = parts[k - h][1] if inside else zero
        col = lax.broadcasted_iota(jnp.int32, (32, 128), 1)
        row = lax.broadcasted_iota(jnp.int32, (32, 128), 0)
        plane = 2 * (col // 8) + (col // 2) % 2
        for o, (k, f) in enumerate(((0, 0), (1, 0), (0, 1))):
            zhi, zlo = split(p_ref[k])
            for h in range(2):
                pick = (plane == row) & ((col // 4) % 2 == f) & (col % 2 == h)
                pick = jnp.where(pick, 1.0, 0.0).astype(BF16)
                hi, lo = dot(zhi, pick).astype(BF16), dot(zlo, pick).astype(BF16)
                at = 64 * o + 32 * h
                z_ref[at : at + 32, 0:128] = hi
                z_ref[at : at + 32, 128:256] = hi
                z_ref[192 + at : 192 + at + 32, 0:128] = lo
                z_ref[192 + at : 192 + at + 32, 128:256] = jnp.zeros_like(lo)


def operators(stream_ops, normal_ops, span_ops):
    wspec = pl.BlockSpec((3, 1, 256, 128), lambda f, k: (0, f, 0, k))
    whole = lambda *shape: pl.BlockSpec(shape, lambda f, k: (0,) * len(shape))
    return pl.pallas_call(
        operators_kernel,
        out_shape=(
            jax.ShapeDtypeStruct((3, 2, 256, 768), BF16),
            jax.ShapeDtypeStruct((3, 2, 256, 768), BF16),
            jax.ShapeDtypeStruct((2, 512, 256), BF16),
            jax.ShapeDtypeStruct((2, 512, 256), BF16),
            jax.ShapeDtypeStruct((384, 256), BF16),
        ),
        grid=(2, 6),
        in_specs=[
            pl.BlockSpec((1, 768, 128), lambda f, k: (f, 0, k)),
            whole(2, 3, 128, 128),
            whole(2, 32, 32),
        ],
        out_specs=(wspec, wspec, whole(2, 512, 256), whole(2, 512, 256), whole(384, 256)),
        compiler_params=params(24),
        cost_estimate=pl.CostEstimate(flops=20_000_000, bytes_accessed=10 << 20, transcendentals=0),
        name="operators",
    )(normal_ops, stream_ops, span_ops)


def normal_kernel(r_ref, whi_ref, wlo_ref, o_ref, vhi_ref, vlo_ref):
    j, f = pl.program_id(0), pl.program_id(1)

    @pl.when((j == 0) & (f == 0))
    def _():
        for q in range(4):
            hi, lo = split(r_ref[:, 48 * q : 48 * q + 48, :].reshape(768, 128))
            vhi_ref[:, 128 * q : 128 * q + 128] = hi
            vlo_ref[:, 128 * q : 128 * q + 128] = lo

    whi, wlo, vhi, vlo = whi_ref[0, 0], wlo_ref[0, 0], vhi_ref[...], vlo_ref[...]
    out = dot(whi, vhi) + dot(whi, vlo) + dot(wlo, vhi)
    for q in range(4):
        o_ref[pl.ds(8 * j + 4 * f + q, 256, stride=24), :] = out[:, 128 * q : 128 * q + 128]


def normal(received, whi, wlo):
    wspec = pl.BlockSpec((1, 1, 256, 768), lambda j, f: (j, f, 0, 0))
    return pl.pallas_call(
        normal_kernel,
        out_shape=jax.ShapeDtypeStruct((256 * 24, 128), F32),
        grid=(3, 2),
        in_specs=[pl.BlockSpec((16, 192, 128), lambda j, f: (0, 0, 0)), wspec, wspec],
        out_specs=pl.BlockSpec((256 * 24, 128), lambda j, f: (0, 0)),
        scratch_shapes=[pltpu.VMEM((768, 512), BF16), pltpu.VMEM((768, 512), BF16)],
        compiler_params=params(32),
        cost_estimate=pl.CostEstimate(flops=3_600_000_000, bytes_accessed=9 << 20, transcendentals=0),
        name="normal",
    )(received, whi, wlo)


def planes_kernel(r_ref, z_ref, bhi_ref, blo_ref, o0_ref, o1_ref, o2_ref, shi_ref, slo_ref):
    zcat = z_ref[...]
    for p in range(8):
        both = []
        for r in (2 * p, 2 * p + 1):
            hi, lo = split(r_ref[16 * r : 16 * r + 16].reshape(128, 128))
            both.append(jnp.concatenate([hi, lo], axis=0))
        t = dot(zcat, jnp.concatenate(both, axis=1))
        t = t[:192] + t[192:]
        for i, r in enumerate((2 * p, 2 * p + 1)):
            here = slice(32 * r, 32 * r + 32)
            before = slice(32 * ((r - 1) % 16), 32 * ((r - 1) % 16) + 32)
            after = slice(32 * ((r + 1) % 16), 32 * ((r + 1) % 16) + 32)
            for o in range(3):
                lanes = slice(128 * i, 128 * i + 128)
                for ref, even, odd in zip(
                    (shi_ref, slo_ref),
                    split(t[64 * o : 64 * o + 32, lanes]),
                    split(t[64 * o + 32 : 64 * o + 64, lanes]),
                ):
                    ref[o, here, 128:256] = even
                    ref[o, before, 384:512] = even
                    ref[o, here, 256:384] = odd
                    ref[o, after, 0:128] = odd
    for o, (op, out_ref) in enumerate(((1, o0_ref), (0, o2_ref), (0, o1_ref))):
        shi, slo, bhi, blo = shi_ref[o], slo_ref[o], bhi_ref[op], blo_ref[op]
        out = dot(shi, bhi) + dot(slo, bhi) + dot(shi, blo)
        for r in range(16):
            out_ref[0, :, 256 * r : 256 * r + 256] = out[32 * r : 32 * r + 32]


def planes(received, zcat, bhi, blo):
    whole = lambda *shape: pl.BlockSpec(shape, lambda j: (0,) * len(shape))
    ospec = pl.BlockSpec((1, 32, 4096), lambda j: (j, 0, 0))
    return pl.pallas_call(
        planes_kernel,
        out_shape=(jax.ShapeDtypeStruct((3, 32, 4096), F32),) * 3,
        grid=(3,),
        in_specs=[
            pl.BlockSpec((256, 8, 128), lambda j: (0, j, 0)),
            whole(384, 256),
            whole(2, 512, 256),
            whole(2, 512, 256),
        ],
        out_specs=(ospec,) * 3,
        scratch_shapes=[pltpu.VMEM((3, 512, 512), BF16), pltpu.VMEM((3, 512, 512), BF16)],
        compiler_params=params(32),
        cost_estimate=pl.CostEstimate(flops=4_500_000_000, bytes_accessed=8 << 20, transcendentals=0),
        name="planes",
    )(received, zcat, bhi, blo)


def per_device(velocity, stream_ops, normal_ops, span_ops):
    whi, wlo, bhi, blo, zcat = operators(stream_ops, normal_ops, span_ops)
    lines = lax.all_to_all(pack(velocity), "row", split_axis=0, concat_axis=0, tiled=True)
    fields = normal(lines, whi, wlo).reshape(256, 24, 128)
    fields = lax.all_to_all(fields, ("row", "col"), split_axis=0, concat_axis=0, tiled=True)
    grads = planes(fields, zcat, bhi, blo)
    return tuple(g.transpose(1, 0, 2) for g in grads)


def solution(mesh):
    return jax.shard_map(
        per_device,
        mesh=mesh,
        in_specs=(P("col", "row", None), P(), P(), P()),
        out_specs=(P(None, ("row", "col"), None),) * 3,
        check_vma=False,
    )
```

```python
import jax
import jax.numpy as jnp
from jax import lax
from jax.experimental import pallas as pl
from jax.experimental.pallas import tpu as pltpu
from jax.sharding import PartitionSpec as P

F32 = jnp.float32
BF16 = jnp.bfloat16


def split(x):
    hi = x.astype(BF16)
    return hi, (x - hi.astype(F32)).astype(BF16)


def dot(a, b):
    return jnp.dot(a, b, preferred_element_type=F32)


def in_hbm(x):
    return pltpu.with_memory_space_constraint(x, pltpu.HBM)


def params(mib):
    return pltpu.CompilerParams(vmem_limit_bytes=mib << 20)


def pack_kernel(v_ref, o_ref):
    for d in range(o_ref.shape[0]):
        for q in range(4):
            z, h = q // 2, q % 2
            o_ref[d, 48 * q : 48 * q + 48, :] = v_ref[z, :, 256 * d + 128 * h : 256 * d + 128 * h + 128]


def pack(velocity):
    steps = 4
    return pl.pallas_call(
        pack_kernel,
        out_shape=jax.ShapeDtypeStruct((16, 192, 128), F32),
        grid=(steps,),
        in_specs=[pl.BlockSpec((2, 48, 4096 // steps), lambda i: (0, 0, i))],
        out_specs=pl.BlockSpec((16 // steps, 192, 128), lambda i: (i, 0, 0)),
        compiler_params=params(61),
        cost_estimate=pl.CostEstimate(flops=0, bytes_accessed=3 << 20, transcendentals=0),
        name="pack",
    )(velocity)


def operators_kernel(n_ref, s_ref, p_ref, whi_ref, wlo_ref, bhi_ref, blo_ref, z_ref):
    for j in range(3):
        whi_ref[j, 0], wlo_ref[j, 0] = split(n_ref[0, pl.ds(j, 256, stride=3), :])

    @pl.when((pl.program_id(0) == 0) & (pl.program_id(1) == 0))
    def _():
        zero = jnp.zeros((128, 128), BF16)
        for op in range(2):
            parts = [split(s_ref[op, d].T) for d in range(3)]
            for k in range(4):
                for h in range(2):
                    inside = 0 <= k - h <= 2
                    rows, lanes = slice(128 * k, 128 * k + 128), slice(128 * h, 128 * h + 128)
                    bhi_ref[op, rows, lanes] = parts[k - h][0] if inside else zero
                    blo_ref[op, rows, lanes] = parts[k - h][1] if inside else zero
        col = lax.broadcasted_iota(jnp.int32, (32, 128), 1)
        row = lax.broadcasted_iota(jnp.int32, (32, 128), 0)
        plane = 2 * (col // 8) + (col // 2) % 2
        for o, (k, f) in enumerate(((0, 0), (1, 0), (0, 1))):
            zhi, zlo = split(p_ref[k])
            for h in range(2):
                pick = (plane == row) & ((col // 4) % 2 == f) & (col % 2 == h)
                pick = jnp.where(pick, 1.0, 0.0).astype(BF16)
                hi, lo = dot(zhi, pick).astype(BF16), dot(zlo, pick).astype(BF16)
                at = 64 * o + 32 * h
                z_ref[at : at + 32, 0:128] = hi
                z_ref[at : at + 32, 128:256] = hi
                z_ref[192 + at : 192 + at + 32, 0:128] = lo
                z_ref[192 + at : 192 + at + 32, 128:256] = jnp.zeros_like(lo)


def operators(stream_ops, normal_ops, span_ops):
    wspec = pl.BlockSpec((3, 1, 256, 128), lambda f, k: (0, f, 0, k))
    whole = lambda *shape: pl.BlockSpec(shape, lambda f, k: (0,) * len(shape))
    return pl.pallas_call(
        operators_kernel,
        out_shape=(
            jax.ShapeDtypeStruct((3, 2, 256, 768), BF16),
            jax.ShapeDtypeStruct((3, 2, 256, 768), BF16),
            jax.ShapeDtypeStruct((2, 512, 256), BF16),
            jax.ShapeDtypeStruct((2, 512, 256), BF16),
            jax.ShapeDtypeStruct((384, 256), BF16),
        ),
        grid=(2, 6),
        in_specs=[
            pl.BlockSpec((1, 768, 128), lambda f, k: (f, 0, k)),
            whole(2, 3, 128, 128),
            whole(2, 32, 32),
        ],
        out_specs=(wspec, wspec, whole(2, 512, 256), whole(2, 512, 256), whole(384, 256)),
        compiler_params=params(61),
        cost_estimate=pl.CostEstimate(flops=20_000_000, bytes_accessed=10 << 20, transcendentals=0),
        name="operators",
    )(normal_ops, stream_ops, span_ops)


def normal_kernel(r_ref, whi_ref, wlo_ref, o_ref, vhi_ref, vlo_ref):
    j, f = pl.program_id(0), pl.program_id(1)

    @pl.when((j == 0) & (f == 0))
    def _():
        for q in range(4):
            hi, lo = split(r_ref[:, 48 * q : 48 * q + 48, :].reshape(768, 128))
            vhi_ref[:, 128 * q : 128 * q + 128] = hi
            vlo_ref[:, 128 * q : 128 * q + 128] = lo

    whi, wlo, vhi, vlo = whi_ref[0, 0], wlo_ref[0, 0], vhi_ref[...], vlo_ref[...]
    out = dot(whi, vhi) + dot(whi, vlo) + dot(wlo, vhi)
    rows = o_ref.reshape(2048, 128)
    for q in range(4):
        rows[pl.ds(4 * f + q, 256, stride=8), :] = out[:, 128 * q : 128 * q + 128]


def normal(received, whi, wlo):
    wspec = pl.BlockSpec((1, 1, 256, 768), lambda j, f: (j, f, 0, 0))
    return pl.pallas_call(
        normal_kernel,
        out_shape=jax.ShapeDtypeStruct((256, 24, 128), F32),
        grid=(3, 2),
        in_specs=[pl.BlockSpec((16, 192, 128), lambda j, f: (0, 0, 0)), wspec, wspec],
        out_specs=pl.BlockSpec((256, 8, 128), lambda j, f: (0, j, 0)),
        scratch_shapes=[pltpu.VMEM((768, 512), BF16), pltpu.VMEM((768, 512), BF16)],
        compiler_params=params(32),
        cost_estimate=pl.CostEstimate(flops=3_600_000_000, bytes_accessed=9 << 20, transcendentals=0),
        name="normal",
    )(received, in_hbm(whi), in_hbm(wlo))


def planes_kernel(r_ref, z_ref, bhi_ref, blo_ref, o0_ref, o1_ref, o2_ref, shi_ref, slo_ref):
    zcat = z_ref[...]
    for p in range(8):
        both = []
        for r in (2 * p, 2 * p + 1):
            hi, lo = split(r_ref[16 * r : 16 * r + 16].reshape(128, 128))
            both.append(jnp.concatenate([hi, lo], axis=0))
        t = dot(zcat, jnp.concatenate(both, axis=1))
        t = t[:192] + t[192:]
        for i, r in enumerate((2 * p, 2 * p + 1)):
            here = slice(32 * r, 32 * r + 32)
            before = slice(32 * ((r - 1) % 16), 32 * ((r - 1) % 16) + 32)
            after = slice(32 * ((r + 1) % 16), 32 * ((r + 1) % 16) + 32)
            for o in range(3):
                lanes = slice(128 * i, 128 * i + 128)
                for ref, even, odd in zip(
                    (shi_ref, slo_ref),
                    split(t[64 * o : 64 * o + 32, lanes]),
                    split(t[64 * o + 32 : 64 * o + 64, lanes]),
                ):
                    ref[o, here, 128:256] = even
                    ref[o, before, 384:512] = even
                    ref[o, here, 256:384] = odd
                    ref[o, after, 0:128] = odd
    for o, (op, out_ref) in enumerate(((1, o0_ref), (0, o2_ref), (0, o1_ref))):
        shi, slo, bhi, blo = shi_ref[o], slo_ref[o], bhi_ref[op], blo_ref[op]
        out = dot(shi, bhi) + dot(slo, bhi) + dot(shi, blo)
        for r in range(16):
            out_ref[0, :, 256 * r : 256 * r + 256] = out[32 * r : 32 * r + 32]


def planes(received, zcat, bhi, blo):
    whole = lambda *shape: pl.BlockSpec(shape, lambda j: (0,) * len(shape))
    ospec = pl.BlockSpec((1, 32, 4096), lambda j: (j, 0, 0))
    return pl.pallas_call(
        planes_kernel,
        out_shape=(jax.ShapeDtypeStruct((3, 32, 4096), F32),) * 3,
        grid=(3,),
        in_specs=[
            pl.BlockSpec((256, 8, 128), lambda j: (0, j, 0)),
            whole(384, 256),
            whole(2, 512, 256),
            whole(2, 512, 256),
        ],
        out_specs=(ospec,) * 3,
        scratch_shapes=[pltpu.VMEM((3, 512, 512), BF16), pltpu.VMEM((3, 512, 512), BF16)],
        compiler_params=params(32),
        cost_estimate=pl.CostEstimate(flops=4_500_000_000, bytes_accessed=8 << 20, transcendentals=0),
        name="planes",
    )(received, zcat, bhi, blo)


def per_device(velocity, stream_ops, normal_ops, span_ops):
    whi, wlo, bhi, blo, zcat = operators(stream_ops, normal_ops, span_ops)
    lines = lax.all_to_all(pack(velocity), "row", split_axis=0, concat_axis=0, tiled=True)
    fields = normal(lines, whi, wlo)
    fields = lax.all_to_all(fields, ("row", "col"), split_axis=0, concat_axis=0, tiled=True)
    grads = planes(fields, zcat, bhi, blo)
    return tuple(g.transpose(1, 0, 2) for g in grads)


def solution(mesh):
    return jax.shard_map(
        per_device,
        mesh=mesh,
        in_specs=(P("col", "row", None), P(), P(), P()),
        out_specs=(P(None, ("row", "col"), None),) * 3,
        check_vma=False,
    )
```

```python
import jax
import jax.numpy as jnp
from jax import lax
from jax.experimental import pallas as pl
from jax.experimental.pallas import tpu as pltpu
from jax.sharding import PartitionSpec as P

F32 = jnp.float32
BF16 = jnp.bfloat16


def split(x):
    hi = x.astype(BF16)
    return hi, (x - hi.astype(F32)).astype(BF16)


def dot(a, b):
    return jnp.dot(a, b, preferred_element_type=F32)


def in_hbm(x):
    return pltpu.with_memory_space_constraint(x, pltpu.HBM)


def params(mib):
    return pltpu.CompilerParams(vmem_limit_bytes=mib << 20)


CHUNKS = 8


def pack_kernel(v_ref, o_ref, in_ref, out_ref, in_sem, out_sem):
    width, blocks = 4096 // CHUNKS, 16 // CHUNKS
    loads = [
        pltpu.make_async_copy(v_ref.at[:, :, pl.ds(width * i, width)], in_ref.at[i], in_sem.at[i])
        for i in range(CHUNKS)
    ]
    stores = [
        pltpu.make_async_copy(
            out_ref.at[pl.ds(blocks * i, blocks)], o_ref.at[pl.ds(blocks * i, blocks)], out_sem.at[i]
        )
        for i in range(CHUNKS)
    ]
    for load in loads:
        load.start()
    for i in range(CHUNKS):
        loads[i].wait()
        for d in range(blocks):
            for q in range(4):
                z, h = q // 2, q % 2
                lanes = slice(256 * d + 128 * h, 256 * d + 128 * h + 128)
                out_ref[blocks * i + d, 48 * q : 48 * q + 48, :] = in_ref[i, z, :, lanes]
        stores[i].start()
    for store in stores:
        store.wait()


def pack(velocity):
    return pl.pallas_call(
        pack_kernel,
        out_shape=jax.ShapeDtypeStruct((16, 192, 128), F32),
        in_specs=[pl.BlockSpec(memory_space=pltpu.HBM)],
        out_specs=pl.BlockSpec(memory_space=pltpu.HBM),
        scratch_shapes=[
            pltpu.VMEM((CHUNKS, 2, 48, 4096 // CHUNKS), F32),
            pltpu.VMEM((16, 192, 128), F32),
            pltpu.SemaphoreType.DMA((CHUNKS,)),
            pltpu.SemaphoreType.DMA((CHUNKS,)),
        ],
        compiler_params=params(32),
        cost_estimate=pl.CostEstimate(flops=0, bytes_accessed=3 << 20, transcendentals=0),
        name="pack",
    )(in_hbm(velocity))


def operators_kernel(n_ref, s_ref, p_ref, whi_ref, wlo_ref, bhi_ref, blo_ref, z_ref):
    for j in range(3):
        whi_ref[j, 0], wlo_ref[j, 0] = split(n_ref[0, pl.ds(j, 256, stride=3), :])

    @pl.when((pl.program_id(0) == 0) & (pl.program_id(1) == 0))
    def _():
        zero = jnp.zeros((128, 128), BF16)
        for op in range(2):
            parts = [split(s_ref[op, d].T) for d in range(3)]
            for k in range(4):
                for h in range(2):
                    inside = 0 <= k - h <= 2
                    rows, lanes = slice(128 * k, 128 * k + 128), slice(128 * h, 128 * h + 128)
                    bhi_ref[op, rows, lanes] = parts[k - h][0] if inside else zero
                    blo_ref[op, rows, lanes] = parts[k - h][1] if inside else zero
        col = lax.broadcasted_iota(jnp.int32, (32, 128), 1)
        row = lax.broadcasted_iota(jnp.int32, (32, 128), 0)
        plane = 2 * (col // 8) + (col // 2) % 2
        for o, (k, f) in enumerate(((0, 0), (1, 0), (0, 1))):
            zhi, zlo = split(p_ref[k])
            for h in range(2):
                pick = (plane == row) & ((col // 4) % 2 == f) & (col % 2 == h)
                pick = jnp.where(pick, 1.0, 0.0).astype(BF16)
                hi, lo = dot(zhi, pick).astype(BF16), dot(zlo, pick).astype(BF16)
                at = 64 * o + 32 * h
                z_ref[at : at + 32, 0:128] = hi
                z_ref[at : at + 32, 128:256] = hi
                z_ref[192 + at : 192 + at + 32, 0:128] = lo
                z_ref[192 + at : 192 + at + 32, 128:256] = jnp.zeros_like(lo)


def operators(stream_ops, normal_ops, span_ops):
    wspec = pl.BlockSpec((3, 1, 256, 128), lambda f, k: (0, f, 0, k))
    whole = lambda *shape: pl.BlockSpec(shape, lambda f, k: (0,) * len(shape))
    return pl.pallas_call(
        operators_kernel,
        out_shape=(
            jax.ShapeDtypeStruct((3, 2, 256, 768), BF16),
            jax.ShapeDtypeStruct((3, 2, 256, 768), BF16),
            jax.ShapeDtypeStruct((2, 512, 256), BF16),
            jax.ShapeDtypeStruct((2, 512, 256), BF16),
            jax.ShapeDtypeStruct((384, 256), BF16),
        ),
        grid=(2, 6),
        in_specs=[
            pl.BlockSpec((1, 768, 128), lambda f, k: (f, 0, k)),
            whole(2, 3, 128, 128),
            whole(2, 32, 32),
        ],
        out_specs=(wspec, wspec, whole(2, 512, 256), whole(2, 512, 256), whole(384, 256)),
        compiler_params=params(61),
        cost_estimate=pl.CostEstimate(flops=20_000_000, bytes_accessed=10 << 20, transcendentals=0),
        name="operators",
    )(normal_ops, stream_ops, span_ops)


def normal_kernel(r_ref, whi_hbm, wlo_hbm, o_ref, vhi_ref, vlo_ref, whi_ref, wlo_ref, sem):
    def copies(t):
        return (
            pltpu.make_async_copy(whi_hbm.at[t], whi_ref.at[t], sem.at[0, t]),
            pltpu.make_async_copy(wlo_hbm.at[t], wlo_ref.at[t], sem.at[1, t]),
        )

    for t in range(6):
        for copy in copies(t):
            copy.start()
    for q in range(4):
        hi, lo = split(r_ref[:, 48 * q : 48 * q + 48, :].reshape(768, 128))
        vhi_ref[:, 128 * q : 128 * q + 128] = hi
        vlo_ref[:, 128 * q : 128 * q + 128] = lo

    @pl.loop(0, 6)
    def _(t):
        for copy in copies(t):
            copy.wait()
        whi, wlo, vhi, vlo = whi_ref[t], wlo_ref[t], vhi_ref[...], vlo_ref[...]
        out = dot(whi, vhi) + dot(whi, vlo) + dot(wlo, vhi)
        for q in range(4):
            o_ref[pl.ds(4 * t + q, 256, stride=24), :] = out[:, 128 * q : 128 * q + 128]


def normal(received, whi, wlo):
    vmem, hbm = pl.BlockSpec(memory_space=pltpu.VMEM), pl.BlockSpec(memory_space=pltpu.HBM)
    return pl.pallas_call(
        normal_kernel,
        out_shape=jax.ShapeDtypeStruct((256 * 24, 128), F32),
        in_specs=[vmem, hbm, hbm],
        out_specs=vmem,
        scratch_shapes=[
            pltpu.VMEM((768, 512), BF16),
            pltpu.VMEM((768, 512), BF16),
            pltpu.VMEM((6, 256, 768), BF16),
            pltpu.VMEM((6, 256, 768), BF16),
            pltpu.SemaphoreType.DMA((2, 6)),
        ],
        compiler_params=params(40),
        cost_estimate=pl.CostEstimate(flops=3_600_000_000, bytes_accessed=9 << 20, transcendentals=0),
        name="normal",
    )(received, in_hbm(whi.reshape(6, 256, 768)), in_hbm(wlo.reshape(6, 256, 768)))


def planes_kernel(r_ref, z_ref, bhi_ref, blo_ref, *refs):
    hbm, (shi_ref, slo_ref, buf_ref, sem) = refs[:3], refs[3:]
    zcat = z_ref[...]

    def copy(o, j):
        return pltpu.make_async_copy(buf_ref.at[o, j], hbm[o].at[j], sem.at[o, j])

    @pl.loop(0, 3)
    def _(j):
        for p in range(8):
            both = []
            for r in (2 * p, 2 * p + 1):
                tile = r_ref[16 * r : 16 * r + 16, pl.ds(pl.multiple_of(8 * j, 8), 8), :]
                both.append(jnp.concatenate(split(tile.reshape(128, 128)), axis=0))
            t = dot(zcat, jnp.concatenate(both, axis=1))
            t = t[:192] + t[192:]
            for i, r in enumerate((2 * p, 2 * p + 1)):
                here = slice(32 * r, 32 * r + 32)
                before = slice(32 * ((r - 1) % 16), 32 * ((r - 1) % 16) + 32)
                after = slice(32 * ((r + 1) % 16), 32 * ((r + 1) % 16) + 32)
                for o in range(3):
                    lanes = slice(128 * i, 128 * i + 128)
                    for ref, even, odd in zip(
                        (shi_ref, slo_ref),
                        split(t[64 * o : 64 * o + 32, lanes]),
                        split(t[64 * o + 32 : 64 * o + 64, lanes]),
                    ):
                        ref[o, here, 128:256] = even
                        ref[o, before, 384:512] = even
                        ref[o, here, 256:384] = odd
                        ref[o, after, 0:128] = odd
        for o, op, at in ((0, 1, 0), (2, 0, 1), (1, 0, 2)):
            shi, slo, bhi, blo = shi_ref[o], slo_ref[o], bhi_ref[op], blo_ref[op]
            out = dot(shi, bhi) + dot(slo, bhi) + dot(shi, blo)
            for r in range(16):
                buf_ref[at, j, :, 256 * r : 256 * r + 256] = out[32 * r : 32 * r + 32]
            copy(at, j).start()

    for o in range(3):
        for j in range(3):
            copy(o, j).wait()


def planes(received, zcat, bhi, blo):
    vmem, hbm = pl.BlockSpec(memory_space=pltpu.VMEM), pl.BlockSpec(memory_space=pltpu.HBM)
    return pl.pallas_call(
        planes_kernel,
        out_shape=(jax.ShapeDtypeStruct((3, 32, 4096), F32),) * 3,
        in_specs=[vmem] * 4,
        out_specs=(hbm,) * 3,
        scratch_shapes=[
            pltpu.VMEM((3, 512, 512), BF16),
            pltpu.VMEM((3, 512, 512), BF16),
            pltpu.VMEM((3, 3, 32, 4096), F32),
            pltpu.SemaphoreType.DMA((3, 3)),
        ],
        compiler_params=params(32),
        cost_estimate=pl.CostEstimate(flops=4_500_000_000, bytes_accessed=8 << 20, transcendentals=0),
        name="planes",
    )(received, zcat, bhi, blo)


def per_device(velocity, stream_ops, normal_ops, span_ops):
    whi, wlo, bhi, blo, zcat = operators(stream_ops, normal_ops, span_ops)
    lines = lax.all_to_all(pack(velocity), "row", split_axis=0, concat_axis=0, tiled=True)
    fields = normal(lines, whi, wlo).reshape(256, 24, 128)
    fields = lax.all_to_all(fields, ("row", "col"), split_axis=0, concat_axis=0, tiled=True)
    grads = planes(fields, zcat, bhi, blo)
    return tuple(g.transpose(1, 0, 2) for g in grads)


def solution(mesh):
    return jax.shard_map(
        per_device,
        mesh=mesh,
        in_specs=(P("col", "row", None), P(), P(), P()),
        out_specs=(P(None, ("row", "col"), None),) * 3,
        check_vma=False,
    )
```

```python
import jax
import jax.numpy as jnp
from jax import lax
from jax.experimental import pallas as pl
from jax.experimental.pallas import tpu as pltpu
from jax.sharding import PartitionSpec as P

F32 = jnp.float32
BF16 = jnp.bfloat16


def split(x):
    hi = x.astype(BF16)
    return hi, (x - hi.astype(F32)).astype(BF16)


def dot(a, b):
    return jnp.dot(a, b, preferred_element_type=F32)


def in_hbm(x):
    return pltpu.with_memory_space_constraint(x, pltpu.HBM)


def params(mib):
    return pltpu.CompilerParams(vmem_limit_bytes=mib << 20)


CHUNKS = 8


def pack_kernel(v_ref, o_ref, in_ref, sem):
    width, blocks = 4096 // CHUNKS, 16 // CHUNKS
    loads = [
        pltpu.make_async_copy(v_ref.at[:, :, pl.ds(width * i, width)], in_ref.at[i], sem.at[i])
        for i in range(CHUNKS)
    ]
    for load in loads:
        load.start()
    for i in range(CHUNKS):
        loads[i].wait()
        for d in range(blocks):
            for q in range(4):
                z, h = q // 2, q % 2
                lanes = slice(256 * d + 128 * h, 256 * d + 128 * h + 128)
                o_ref[blocks * i + d, 48 * q : 48 * q + 48, :] = in_ref[i, z, :, lanes]


def pack(velocity):
    return pl.pallas_call(
        pack_kernel,
        out_shape=jax.ShapeDtypeStruct((16, 192, 128), F32),
        in_specs=[pl.BlockSpec(memory_space=pltpu.HBM)],
        out_specs=pl.BlockSpec(memory_space=pltpu.VMEM),
        scratch_shapes=[
            pltpu.VMEM((CHUNKS, 2, 48, 4096 // CHUNKS), F32),
            pltpu.SemaphoreType.DMA((CHUNKS,)),
        ],
        compiler_params=params(8),
        cost_estimate=pl.CostEstimate(flops=0, bytes_accessed=3 << 20, transcendentals=0),
        name="pack",
    )(in_hbm(velocity))


def operators(s_ref, p_ref, bhi_ref, blo_ref, z_ref):
    zero = jnp.zeros((128, 128), BF16)
    for op in range(2):
        parts = [split(s_ref[op, d].T) for d in range(3)]
        for k in range(4):
            for h in range(2):
                inside = 0 <= k - h <= 2
                rows, lanes = slice(128 * k, 128 * k + 128), slice(128 * h, 128 * h + 128)
                bhi_ref[op, rows, lanes] = parts[k - h][0] if inside else zero
                blo_ref[op, rows, lanes] = parts[k - h][1] if inside else zero
    col = lax.broadcasted_iota(jnp.int32, (32, 128), 1)
    row = lax.broadcasted_iota(jnp.int32, (32, 128), 0)
    plane = 2 * (col // 8) + (col // 2) % 2
    for o, (k, f) in enumerate(((0, 0), (1, 0), (0, 1))):
        zhi, zlo = split(p_ref[k])
        for h in range(2):
            pick = (plane == row) & ((col // 4) % 2 == f) & (col % 2 == h)
            pick = jnp.where(pick, 1.0, 0.0).astype(BF16)
            hi, lo = dot(zhi, pick).astype(BF16), dot(zlo, pick).astype(BF16)
            at = 64 * o + 32 * h
            z_ref[at : at + 32, 0:128] = hi
            z_ref[at : at + 32, 128:256] = hi
            z_ref[192 + at : 192 + at + 32, 0:128] = lo
            z_ref[192 + at : 192 + at + 32, 128:256] = jnp.zeros_like(lo)


def normal_kernel(r_ref, n_ref, s_ref, p_ref, o_ref, bhi_ref, blo_ref, z_ref, vhi_ref, vlo_ref):
    for q in range(4):
        hi, lo = split(r_ref[:, 48 * q : 48 * q + 48, :].reshape(768, 128))
        vhi_ref[:, 128 * q : 128 * q + 128] = hi
        vlo_ref[:, 128 * q : 128 * q + 128] = lo

    for f in range(2):

        @pl.loop(0, 3)
        def _(t):
            at = pl.multiple_of(256 * t, 256)
            whi, wlo = split(n_ref[f, pl.ds(at, 256), :])
            vhi, vlo = vhi_ref[...], vlo_ref[...]
            out = dot(whi, vhi) + dot(whi, vlo) + dot(wlo, vhi)
            for q in range(4):
                o_ref[pl.ds(8 * at + 4 * f + q, 256, stride=8), :] = out[:, 128 * q : 128 * q + 128]

    operators(s_ref, p_ref, bhi_ref, blo_ref, z_ref)


def normal(received, stream_ops, normal_ops, span_ops):
    vmem = pl.BlockSpec(memory_space=pltpu.VMEM)
    return pl.pallas_call(
        normal_kernel,
        out_shape=(
            jax.ShapeDtypeStruct((256 * 24, 128), F32),
            jax.ShapeDtypeStruct((2, 512, 256), BF16),
            jax.ShapeDtypeStruct((2, 512, 256), BF16),
            jax.ShapeDtypeStruct((384, 256), BF16),
        ),
        in_specs=[vmem] * 4,
        out_specs=(vmem,) * 4,
        scratch_shapes=[pltpu.VMEM((768, 512), BF16), pltpu.VMEM((768, 512), BF16)],
        compiler_params=params(24),
        cost_estimate=pl.CostEstimate(flops=3_600_000_000, bytes_accessed=9 << 20, transcendentals=0),
        name="normal",
    )(received, normal_ops, stream_ops, span_ops)


def planes_kernel(r_ref, z_ref, bhi_ref, blo_ref, *refs):
    hbm, (shi_ref, slo_ref, buf_ref, sem) = refs[:3], refs[3:]
    zcat = z_ref[...]

    def copy(o, j):
        return pltpu.make_async_copy(buf_ref.at[o, j], hbm[o].at[j], sem.at[o, j])

    @pl.loop(0, 3)
    def _(j):
        for p in range(8):
            both = []
            for r in (2 * p, 2 * p + 1):
                tile = r_ref[16 * r : 16 * r + 16, pl.ds(pl.multiple_of(8 * j, 8), 8), :]
                both.append(jnp.concatenate(split(tile.reshape(128, 128)), axis=0))
            t = dot(zcat, jnp.concatenate(both, axis=1))
            t = t[:192] + t[192:]
            for i, r in enumerate((2 * p, 2 * p + 1)):
                here = slice(32 * r, 32 * r + 32)
                before = slice(32 * ((r - 1) % 16), 32 * ((r - 1) % 16) + 32)
                after = slice(32 * ((r + 1) % 16), 32 * ((r + 1) % 16) + 32)
                for o in range(3):
                    lanes = slice(128 * i, 128 * i + 128)
                    for ref, even, odd in zip(
                        (shi_ref, slo_ref),
                        split(t[64 * o : 64 * o + 32, lanes]),
                        split(t[64 * o + 32 : 64 * o + 64, lanes]),
                    ):
                        ref[o, here, 128:256] = even
                        ref[o, before, 384:512] = even
                        ref[o, here, 256:384] = odd
                        ref[o, after, 0:128] = odd
        for o, op, at in ((0, 1, 0), (2, 0, 1), (1, 0, 2)):
            shi, slo, bhi, blo = shi_ref[o], slo_ref[o], bhi_ref[op], blo_ref[op]
            out = dot(shi, bhi) + dot(slo, bhi) + dot(shi, blo)
            for r in range(16):
                buf_ref[at, j, :, 256 * r : 256 * r + 256] = out[32 * r : 32 * r + 32]
            copy(at, j).start()

    for o in range(3):
        for j in range(3):
            copy(o, j).wait()


def planes(received, zcat, bhi, blo):
    vmem, hbm = pl.BlockSpec(memory_space=pltpu.VMEM), pl.BlockSpec(memory_space=pltpu.HBM)
    return pl.pallas_call(
        planes_kernel,
        out_shape=(jax.ShapeDtypeStruct((3, 32, 4096), F32),) * 3,
        in_specs=[vmem] * 4,
        out_specs=(hbm,) * 3,
        scratch_shapes=[
            pltpu.VMEM((3, 512, 512), BF16),
            pltpu.VMEM((3, 512, 512), BF16),
            pltpu.VMEM((3, 3, 32, 4096), F32),
            pltpu.SemaphoreType.DMA((3, 3)),
        ],
        compiler_params=params(32),
        cost_estimate=pl.CostEstimate(flops=4_500_000_000, bytes_accessed=8 << 20, transcendentals=0),
        name="planes",
    )(received, zcat, bhi, blo)


def per_device(velocity, stream_ops, normal_ops, span_ops):
    lines = lax.all_to_all(pack(velocity), "row", split_axis=0, concat_axis=0, tiled=True)
    fields, bhi, blo, zcat = normal(lines, stream_ops, normal_ops, span_ops)
    fields = fields.reshape(256, 24, 128)
    fields = lax.all_to_all(fields, ("row", "col"), split_axis=0, concat_axis=0, tiled=True)
    grads = planes(fields, zcat, bhi, blo)
    return tuple(g.transpose(1, 0, 2) for g in grads)


def solution(mesh):
    return jax.shard_map(
        per_device,
        mesh=mesh,
        in_specs=(P("col", "row", None), P(), P(), P()),
        out_specs=(P(None, ("row", "col"), None),) * 3,
        check_vma=False,
    )
```

```python
import jax
import jax.numpy as jnp
from jax import lax
from jax.experimental import pallas as pl
from jax.experimental.pallas import tpu as pltpu
from jax.sharding import PartitionSpec as P

F32 = jnp.float32
BF16 = jnp.bfloat16


def split(x):
    hi = x.astype(BF16)
    return hi, (x - hi.astype(F32)).astype(BF16)


def dot(a, b):
    return jnp.dot(a, b, preferred_element_type=F32)


def in_hbm(x):
    return pltpu.with_memory_space_constraint(x, pltpu.HBM)


def params(mib):
    return pltpu.CompilerParams(vmem_limit_bytes=mib << 20)


CHUNKS = 8


def pack_kernel(v_ref, o_ref, in_ref, sem):
    width, blocks = 4096 // CHUNKS, 16 // CHUNKS
    loads = [
        pltpu.make_async_copy(v_ref.at[:, :, pl.ds(width * i, width)], in_ref.at[i], sem.at[i])
        for i in range(CHUNKS)
    ]
    for load in loads:
        load.start()
    for i in range(CHUNKS):
        loads[i].wait()
        for d in range(blocks):
            for q in range(4):
                z, h = q // 2, q % 2
                lanes = slice(256 * d + 128 * h, 256 * d + 128 * h + 128)
                o_ref[blocks * i + d, 48 * q : 48 * q + 48, :] = in_ref[i, z, :, lanes]


def pack(velocity):
    return pl.pallas_call(
        pack_kernel,
        out_shape=jax.ShapeDtypeStruct((16, 192, 128), F32),
        in_specs=[pl.BlockSpec(memory_space=pltpu.HBM)],
        out_specs=pl.BlockSpec(memory_space=pltpu.VMEM),
        scratch_shapes=[
            pltpu.VMEM((CHUNKS, 2, 48, 4096 // CHUNKS), F32),
            pltpu.SemaphoreType.DMA((CHUNKS,)),
        ],
        compiler_params=params(8),
        cost_estimate=pl.CostEstimate(flops=0, bytes_accessed=3 << 20, transcendentals=0),
        name="pack",
    )(in_hbm(velocity))


def operators(s_ref, p_ref, b_ref, z_ref):
    zero = jnp.zeros((128, 128), BF16)
    for op in range(2):
        (lhi, llo), (ohi, olo), (rhi, rlo) = (split(s_ref[op, d].T) for d in range(3))
        tiles = (
            ((ohi, lhi), (rhi, ohi)),
            ((olo, llo), (rlo, olo)),
            ((lhi, llo), (lhi, zero)),
            ((rhi, rlo), (rhi, zero)),
        )
        for t, tile in enumerate(tiles):
            for k in range(2):
                for h in range(2):
                    b_ref[op, t, 128 * k : 128 * k + 128, 128 * h : 128 * h + 128] = tile[k][h]
    col = lax.broadcasted_iota(jnp.int32, (32, 256), 1)
    row = lax.broadcasted_iota(jnp.int32, (32, 256), 0)
    plane = 2 * (col % 16) + (col // 32) % 2
    for o, k in enumerate((0, 1, 0)):
        zhi, zlo = split(p_ref[k])
        for h in range(2):
            pick = jnp.where((plane == row) & ((col // 16) % 2 == h), 1.0, 0.0)
            first = jnp.where(col < 128, pick, 0.0).astype(BF16)
            last = jnp.where(col < 128, 0.0, pick).astype(BF16)
            at = 64 * o + 32 * h
            z_ref[at : at + 32, :] = (dot(zhi, first) + dot(zlo, last)).astype(BF16)


def normal_kernel(r_ref, n_ref, s_ref, p_ref, o_ref, b_ref, z_ref, vhi_ref, vlo_ref):
    for q in range(4):
        hi, lo = split(r_ref[:, 48 * q : 48 * q + 48, :].reshape(768, 128))
        vhi_ref[:, 128 * q : 128 * q + 128] = hi
        vlo_ref[:, 128 * q : 128 * q + 128] = lo

    def step(f, at):
        whi, wlo = split(n_ref[f, pl.ds(at, 256), :])
        vhi, vlo = vhi_ref[...], vlo_ref[...]
        out = dot(whi, vhi) + dot(whi, vlo) + dot(wlo, vhi)
        for q in range(4):
            o_ref[pl.ds(8 * at + 4 * f + q, 256, stride=8), :] = out[:, 128 * q : 128 * q + 128]

    for f, steps in ((0, 3), (1, 2)):

        @pl.loop(0, steps)
        def _(t):
            step(f, pl.multiple_of(256 * t, 256))

    operators(s_ref, p_ref, b_ref, z_ref)
    step(1, 512)


def normal(received, stream_ops, normal_ops, span_ops):
    vmem = pl.BlockSpec(memory_space=pltpu.VMEM)
    return pl.pallas_call(
        normal_kernel,
        out_shape=(
            jax.ShapeDtypeStruct((256 * 24, 128), F32),
            jax.ShapeDtypeStruct((2, 4, 256, 256), BF16),
            jax.ShapeDtypeStruct((192, 256), BF16),
        ),
        in_specs=[vmem] * 4,
        out_specs=(vmem,) * 3,
        scratch_shapes=[pltpu.VMEM((768, 512), BF16), pltpu.VMEM((768, 512), BF16)],
        compiler_params=params(24),
        cost_estimate=pl.CostEstimate(flops=3_600_000_000, bytes_accessed=9 << 20, transcendentals=0),
        name="normal",
    )(received, normal_ops, stream_ops, span_ops)


def planes_kernel(r_ref, z_ref, b_ref, *refs):
    hbm, (chi_ref, clo_ref, left_ref, right_ref, buf_ref, sem) = refs[:3], refs[3:]

    def copy(o, j):
        return pltpu.make_async_copy(buf_ref.at[o, j], hbm[o].at[j], sem.at[o, j])

    @pl.loop(0, 3)
    def _(j):
        for p in range(8):
            for f, rows, fields in ((0, slice(0, 128), (0, 1)), (1, slice(128, 192), (2,))):
                both = []
                for r in (2 * p, 2 * p + 1):
                    lines = [r_ref[pl.ds(384 * r + 8 * j + 4 * f + q, 16, stride=24), :] for q in range(4)]
                    both.append(jnp.concatenate(split(jnp.concatenate(lines, axis=0)) * 2, axis=0))
                t = dot(z_ref[rows, :], jnp.concatenate(both, axis=1))
                for i, r in enumerate((2 * p, 2 * p + 1)):
                    here = slice(32 * r, 32 * r + 32)
                    before = slice(32 * ((r - 1) % 16), 32 * ((r - 1) % 16) + 32)
                    after = slice(32 * ((r + 1) % 16), 32 * ((r + 1) % 16) + 32)
                    lanes = slice(128 * i, 128 * i + 128)
                    for n, o in enumerate(fields):
                        hi, lo = split(t[64 * n : 64 * n + 32, lanes])
                        chi_ref[o, here, 0:128] = hi
                        clo_ref[o, here, 0:128] = lo
                        right_ref[o, before, 0:128] = hi
                        right_ref[o, before, 128:256] = lo
                        hi, lo = split(t[64 * n + 32 : 64 * n + 64, lanes])
                        chi_ref[o, here, 128:256] = hi
                        clo_ref[o, here, 128:256] = lo
                        left_ref[o, after, 0:128] = hi
                        left_ref[o, after, 128:256] = lo
        for o, op, at in ((0, 1, 0), (2, 0, 1), (1, 0, 2)):
            chi, clo = chi_ref[o], clo_ref[o]
            out = dot(chi, b_ref[op, 0]) + dot(clo, b_ref[op, 0]) + dot(chi, b_ref[op, 1])
            left, right = dot(left_ref[o], b_ref[op, 2]), dot(right_ref[o], b_ref[op, 3])
            first = out[:, 0:128] + (left[:, 0:128] + left[:, 128:256])
            second = out[:, 128:256] + (right[:, 0:128] + right[:, 128:256])
            for r in range(16):
                buf_ref[at, j, :, 256 * r : 256 * r + 128] = first[32 * r : 32 * r + 32]
                buf_ref[at, j, :, 256 * r + 128 : 256 * r + 256] = second[32 * r : 32 * r + 32]
            copy(at, j).start()

    for o in range(3):
        for j in range(3):
            copy(o, j).wait()


def planes(received, zcat, blocks):
    vmem, hbm = pl.BlockSpec(memory_space=pltpu.VMEM), pl.BlockSpec(memory_space=pltpu.HBM)
    return pl.pallas_call(
        planes_kernel,
        out_shape=(jax.ShapeDtypeStruct((3, 32, 4096), F32),) * 3,
        in_specs=[vmem] * 3,
        out_specs=(hbm,) * 3,
        scratch_shapes=[pltpu.VMEM((3, 512, 256), BF16)] * 4
        + [pltpu.VMEM((3, 3, 32, 4096), F32), pltpu.SemaphoreType.DMA((3, 3))],
        compiler_params=params(32),
        cost_estimate=pl.CostEstimate(flops=4_000_000_000, bytes_accessed=8 << 20, transcendentals=0),
        name="planes",
    )(received.reshape(256 * 24, 128), zcat, blocks)


def per_device(velocity, stream_ops, normal_ops, span_ops):
    lines = lax.all_to_all(pack(velocity), "row", split_axis=0, concat_axis=0, tiled=True)
    fields, blocks, zcat = normal(lines, stream_ops, normal_ops, span_ops)
    fields = fields.reshape(256, 24, 128)
    fields = lax.all_to_all(fields, ("row", "col"), split_axis=0, concat_axis=0, tiled=True)
    grads = planes(fields, zcat, blocks)
    return tuple(g.transpose(1, 0, 2) for g in grads)


def solution(mesh):
    return jax.shard_map(
        per_device,
        mesh=mesh,
        in_specs=(P("col", "row", None), P(), P(), P()),
        out_specs=(P(None, ("row", "col"), None),) * 3,
        check_vma=False,
    )
```

```python
import jax
import jax.numpy as jnp
from jax import lax
from jax.experimental import pallas as pl
from jax.experimental.pallas import tpu as pltpu
from jax.sharding import PartitionSpec as P

F32 = jnp.float32
BF16 = jnp.bfloat16


def split(x):
    hi = x.astype(BF16)
    return hi, (x - hi.astype(F32)).astype(BF16)


def dot(a, b):
    return jnp.dot(a, b, preferred_element_type=F32)


def in_hbm(x):
    return pltpu.with_memory_space_constraint(x, pltpu.HBM)


def params(mib):
    return pltpu.CompilerParams(vmem_limit_bytes=mib << 20)


CHUNKS = 8


def pack_kernel(v_ref, o_ref, in_ref, sem):
    width, blocks = 4096 // CHUNKS, 16 // CHUNKS
    loads = [
        pltpu.make_async_copy(v_ref.at[:, :, pl.ds(width * i, width)], in_ref.at[i], sem.at[i])
        for i in range(CHUNKS)
    ]
    for load in loads:
        load.start()
    for i in range(CHUNKS):
        loads[i].wait()
        for d in range(blocks):
            for q in range(4):
                z, h = q // 2, q % 2
                lanes = slice(256 * d + 128 * h, 256 * d + 128 * h + 128)
                o_ref[blocks * i + d, 48 * q : 48 * q + 48, :] = in_ref[i, z, :, lanes]


def pack(velocity):
    return pl.pallas_call(
        pack_kernel,
        out_shape=jax.ShapeDtypeStruct((16, 192, 128), F32),
        in_specs=[pl.BlockSpec(memory_space=pltpu.HBM)],
        out_specs=pl.BlockSpec(memory_space=pltpu.VMEM),
        scratch_shapes=[
            pltpu.VMEM((CHUNKS, 2, 48, 4096 // CHUNKS), F32),
            pltpu.SemaphoreType.DMA((CHUNKS,)),
        ],
        compiler_params=params(8),
        cost_estimate=pl.CostEstimate(flops=0, bytes_accessed=3 << 20, transcendentals=0),
        name="pack",
    )(in_hbm(velocity))


def operators(s_ref, p_ref, b_ref, z_ref):
    zero = jnp.zeros((128, 128), BF16)
    for op in range(2):
        (lhi, llo), (ohi, olo), (rhi, rlo) = (split(s_ref[op, d].T) for d in range(3))
        tiles = (
            ((ohi, lhi), (rhi, ohi)),
            ((olo, llo), (rlo, olo)),
            ((lhi, llo), (lhi, zero)),
            ((rhi, rlo), (rhi, zero)),
        )
        for t, tile in enumerate(tiles):
            for k in range(2):
                for h in range(2):
                    b_ref[op, t, 128 * k : 128 * k + 128, 128 * h : 128 * h + 128] = tile[k][h]
    col = lax.broadcasted_iota(jnp.int32, (32, 256), 1)
    row = lax.broadcasted_iota(jnp.int32, (32, 256), 0)
    plane = 2 * (col % 16) + (col // 32) % 2
    for o, k in enumerate((0, 1, 0)):
        zhi, zlo = split(p_ref[k])
        for h in range(2):
            pick = jnp.where((plane == row) & ((col // 16) % 2 == h), 1.0, 0.0)
            first = jnp.where(col < 128, pick, 0.0).astype(BF16)
            last = jnp.where(col < 128, 0.0, pick).astype(BF16)
            at = 64 * o + 32 * h
            z_ref[at : at + 32, :] = (dot(zhi, first) + dot(zlo, last)).astype(BF16)


def normal_kernel(r_ref, n_ref, s_ref, p_ref, o_ref, b_ref, z_ref, vhi_ref, vlo_ref):
    for q in range(4):
        hi, lo = split(r_ref[:, 48 * q : 48 * q + 48, :].reshape(768, 128))
        vhi_ref[:, 128 * q : 128 * q + 128] = hi
        vlo_ref[:, 128 * q : 128 * q + 128] = lo

    def step(f, at):
        whi, wlo = split(n_ref[f, pl.ds(at, 256), :])
        vhi, vlo = vhi_ref[...], vlo_ref[...]
        out = dot(whi, vhi) + dot(whi, vlo) + dot(wlo, vhi)
        for q in range(4):
            o_ref[pl.ds(8 * at + 4 * f + q, 256, stride=8), :] = out[:, 128 * q : 128 * q + 128]

    for f, steps in ((0, 3), (1, 2)):

        @pl.loop(0, steps)
        def _(t):
            step(f, pl.multiple_of(256 * t, 256))

    operators(s_ref, p_ref, b_ref, z_ref)
    step(1, 512)


def normal(received, stream_ops, normal_ops, span_ops):
    vmem = pl.BlockSpec(memory_space=pltpu.VMEM)
    return pl.pallas_call(
        normal_kernel,
        out_shape=(
            jax.ShapeDtypeStruct((256 * 24, 128), F32),
            jax.ShapeDtypeStruct((2, 4, 256, 256), BF16),
            jax.ShapeDtypeStruct((192, 256), BF16),
        ),
        in_specs=[vmem] * 4,
        out_specs=(vmem,) * 3,
        scratch_shapes=[pltpu.VMEM((768, 512), BF16), pltpu.VMEM((768, 512), BF16)],
        compiler_params=params(24),
        cost_estimate=pl.CostEstimate(flops=3_600_000_000, bytes_accessed=9 << 20, transcendentals=0),
        name="normal",
    )(received, normal_ops, stream_ops, span_ops)


def planes_kernel(r_ref, z_ref, b_ref, *refs):
    hbm, sets, (buf_ref, sem) = refs[:3], (refs[3:7], refs[7:11]), refs[11:]

    def copy(o, j):
        return pltpu.make_async_copy(buf_ref.at[o, j], hbm[o].at[j], sem.at[o, j])

    def spanwise(j, p):
        chi_ref, clo_ref, left_ref, right_ref = sets[j % 2]
        for f, rows, fields in ((0, slice(0, 128), (0, 1)), (1, slice(128, 192), (2,))):
            both = []
            for r in (2 * p, 2 * p + 1):
                lines = [r_ref[pl.ds(384 * r + 8 * j + 4 * f + q, 16, stride=24), :] for q in range(4)]
                both.append(jnp.concatenate(split(jnp.concatenate(lines, axis=0)) * 2, axis=0))
            t = dot(z_ref[rows, :], jnp.concatenate(both, axis=1))
            for i, r in enumerate((2 * p, 2 * p + 1)):
                here = slice(32 * r, 32 * r + 32)
                before = slice(32 * ((r - 1) % 16), 32 * ((r - 1) % 16) + 32)
                after = slice(32 * ((r + 1) % 16), 32 * ((r + 1) % 16) + 32)
                lanes = slice(128 * i, 128 * i + 128)
                for n, o in enumerate(fields):
                    hi, lo = split(t[64 * n : 64 * n + 32, lanes])
                    chi_ref[o, here, 0:128] = hi
                    clo_ref[o, here, 0:128] = lo
                    right_ref[o, before, 0:128] = hi
                    right_ref[o, before, 128:256] = lo
                    hi, lo = split(t[64 * n + 32 : 64 * n + 64, lanes])
                    chi_ref[o, here, 128:256] = hi
                    clo_ref[o, here, 128:256] = lo
                    left_ref[o, after, 0:128] = hi
                    left_ref[o, after, 128:256] = lo

    def streamwise(j, o, op, at):
        chi_ref, clo_ref, left_ref, right_ref = sets[j % 2]
        chi, clo = chi_ref[o], clo_ref[o]
        out = dot(chi, b_ref[op, 0]) + dot(clo, b_ref[op, 0]) + dot(chi, b_ref[op, 1])
        left, right = dot(left_ref[o], b_ref[op, 2]), dot(right_ref[o], b_ref[op, 3])
        first = out[:, 0:128] + (left[:, 0:128] + left[:, 128:256])
        second = out[:, 128:256] + (right[:, 0:128] + right[:, 128:256])
        for r in range(16):
            buf_ref[at, j, :, 256 * r : 256 * r + 128] = first[32 * r : 32 * r + 32]
            buf_ref[at, j, :, 256 * r + 128 : 256 * r + 256] = second[32 * r : 32 * r + 32]
        copy(at, j).start()

    for p in range(8):
        spanwise(0, p)
    for j in range(3):
        for step, (o, op, at) in enumerate(((0, 1, 0), (2, 0, 1), (1, 0, 2))):
            if j < 2:
                for p in ((0, 1, 2), (3, 4, 5), (6, 7))[step]:
                    spanwise(j + 1, p)
            streamwise(j, o, op, at)

    for o in range(3):
        for j in range(3):
            copy(o, j).wait()


def planes(received, zcat, blocks):
    vmem, hbm = pl.BlockSpec(memory_space=pltpu.VMEM), pl.BlockSpec(memory_space=pltpu.HBM)
    return pl.pallas_call(
        planes_kernel,
        out_shape=(jax.ShapeDtypeStruct((3, 32, 4096), F32),) * 3,
        in_specs=[vmem] * 3,
        out_specs=(hbm,) * 3,
        scratch_shapes=[pltpu.VMEM((3, 512, 256), BF16)] * 8
        + [pltpu.VMEM((3, 3, 32, 4096), F32), pltpu.SemaphoreType.DMA((3, 3))],
        compiler_params=params(32),
        cost_estimate=pl.CostEstimate(flops=4_000_000_000, bytes_accessed=8 << 20, transcendentals=0),
        name="planes",
    )(received.reshape(256 * 24, 128), zcat, blocks)


def per_device(velocity, stream_ops, normal_ops, span_ops):
    lines = lax.all_to_all(pack(velocity), "row", split_axis=0, concat_axis=0, tiled=True)
    fields, blocks, zcat = normal(lines, stream_ops, normal_ops, span_ops)
    fields = fields.reshape(256, 24, 128)
    fields = lax.all_to_all(fields, ("row", "col"), split_axis=0, concat_axis=0, tiled=True)
    grads = planes(fields, zcat, blocks)
    return tuple(g.transpose(1, 0, 2) for g in grads)


def solution(mesh):
    return jax.shard_map(
        per_device,
        mesh=mesh,
        in_specs=(P("col", "row", None), P(), P(), P()),
        out_specs=(P(None, ("row", "col"), None),) * 3,
        check_vma=False,
    )
```

```python
import jax
import jax.numpy as jnp
from jax import lax
from jax.experimental import pallas as pl
from jax.experimental.pallas import tpu as pltpu
from jax.sharding import PartitionSpec as P

F32 = jnp.float32
BF16 = jnp.bfloat16


def split(x):
    hi = x.astype(BF16)
    return hi, (x - hi.astype(F32)).astype(BF16)


def dot(a, b):
    return jnp.dot(a, b, preferred_element_type=F32)


def in_hbm(x):
    return pltpu.with_memory_space_constraint(x, pltpu.HBM)


def params(mib):
    return pltpu.CompilerParams(vmem_limit_bytes=mib << 20)


CHUNKS = 8


def pack_kernel(v_ref, o_ref, in_ref, sem):
    width, blocks = 4096 // CHUNKS, 16 // CHUNKS
    loads = [
        pltpu.make_async_copy(v_ref.at[:, :, pl.ds(width * i, width)], in_ref.at[i], sem.at[i])
        for i in range(CHUNKS)
    ]
    for load in loads:
        load.start()
    for i in range(CHUNKS):
        loads[i].wait()
        for d in range(blocks):
            for q in range(4):
                z, h = q // 2, q % 2
                lanes = slice(256 * d + 128 * h, 256 * d + 128 * h + 128)
                o_ref[blocks * i + d, 48 * q : 48 * q + 48, :] = in_ref[i, z, :, lanes]


def pack(velocity):
    return pl.pallas_call(
        pack_kernel,
        out_shape=jax.ShapeDtypeStruct((16, 192, 128), F32),
        in_specs=[pl.BlockSpec(memory_space=pltpu.HBM)],
        out_specs=pl.BlockSpec(memory_space=pltpu.VMEM),
        scratch_shapes=[
            pltpu.VMEM((CHUNKS, 2, 48, 4096 // CHUNKS), F32),
            pltpu.SemaphoreType.DMA((CHUNKS,)),
        ],
        compiler_params=params(8),
        cost_estimate=pl.CostEstimate(flops=0, bytes_accessed=3 << 20, transcendentals=0),
        name="pack",
    )(in_hbm(velocity))


def operators(s_ref, p_ref, b_ref, z_ref):
    zero = jnp.zeros((128, 128), BF16)
    for op in range(2):
        (lhi, llo), (ohi, olo), (rhi, rlo) = (split(s_ref[op, d].T) for d in range(3))
        tiles = (
            ((ohi, lhi), (rhi, ohi)),
            ((olo, llo), (rlo, olo)),
            ((lhi, llo), (lhi, zero)),
            ((rhi, rlo), (rhi, zero)),
        )
        for t, tile in enumerate(tiles):
            for k in range(2):
                for h in range(2):
                    b_ref[op, t, 128 * k : 128 * k + 128, 128 * h : 128 * h + 128] = tile[k][h]
    col = lax.broadcasted_iota(jnp.int32, (32, 256), 1)
    row = lax.broadcasted_iota(jnp.int32, (32, 256), 0)
    plane = 2 * (col % 16) + (col // 32) % 2
    for o, k in enumerate((0, 1, 0)):
        zhi, zlo = split(p_ref[k])
        for h in range(2):
            pick = jnp.where((plane == row) & ((col // 16) % 2 == h), 1.0, 0.0)
            first = jnp.where(col < 128, pick, 0.0).astype(BF16)
            last = jnp.where(col < 128, 0.0, pick).astype(BF16)
            at = 64 * o + 32 * h
            z_ref[at : at + 32, :] = (dot(zhi, first) + dot(zlo, last)).astype(BF16)


def normal_kernel(r_ref, n_ref, s_ref, p_ref, o_ref, b_ref, z_ref, vhi_ref, vlo_ref):
    for q in range(4):
        hi, lo = split(r_ref[:, 48 * q : 48 * q + 48, :].reshape(768, 128))
        vhi_ref[:, 128 * q : 128 * q + 128] = hi
        vlo_ref[:, 128 * q : 128 * q + 128] = lo

    def step(f, at):
        whi, wlo = split(n_ref[f, pl.ds(at, 256), :])
        vhi, vlo = vhi_ref[...], vlo_ref[...]
        out = dot(whi, vhi) + dot(whi, vlo) + dot(wlo, vhi)
        for q in range(4):
            o_ref[pl.ds(8 * at + 4 * f + q, 256, stride=8), :] = out[:, 128 * q : 128 * q + 128]

    for f in range(2):
        for t in range(3):
            step(f, 256 * t)
            if f == 0 and t == 0:
                operators(s_ref, p_ref, b_ref, z_ref)


def normal(received, stream_ops, normal_ops, span_ops):
    vmem = pl.BlockSpec(memory_space=pltpu.VMEM)
    return pl.pallas_call(
        normal_kernel,
        out_shape=(
            jax.ShapeDtypeStruct((256 * 24, 128), F32),
            jax.ShapeDtypeStruct((2, 4, 256, 256), BF16),
            jax.ShapeDtypeStruct((192, 256), BF16),
        ),
        in_specs=[vmem] * 4,
        out_specs=(vmem,) * 3,
        scratch_shapes=[pltpu.VMEM((768, 512), BF16), pltpu.VMEM((768, 512), BF16)],
        compiler_params=params(24),
        cost_estimate=pl.CostEstimate(flops=3_600_000_000, bytes_accessed=9 << 20, transcendentals=0),
        name="normal",
    )(received, normal_ops, stream_ops, span_ops)


def planes_kernel(r_ref, z_ref, b_ref, *refs):
    hbm, sets, (buf_ref, sem) = refs[:3], (refs[3:7], refs[7:11]), refs[11:]

    def copy(o, j):
        return pltpu.make_async_copy(buf_ref.at[o, j], hbm[o].at[j], sem.at[o, j])

    def spanwise(j, p):
        chi_ref, clo_ref, left_ref, right_ref = sets[j % 2]
        for f, rows, fields in ((0, slice(0, 128), (0, 1)), (1, slice(128, 192), (2,))):
            both = []
            for r in (2 * p, 2 * p + 1):
                lines = [r_ref[pl.ds(384 * r + 8 * j + 4 * f + q, 16, stride=24), :] for q in range(4)]
                both.append(jnp.concatenate(split(jnp.concatenate(lines, axis=0)) * 2, axis=0))
            t = dot(z_ref[rows, :], jnp.concatenate(both, axis=1))
            for i, r in enumerate((2 * p, 2 * p + 1)):
                here = slice(32 * r, 32 * r + 32)
                before = slice(32 * ((r - 1) % 16), 32 * ((r - 1) % 16) + 32)
                after = slice(32 * ((r + 1) % 16), 32 * ((r + 1) % 16) + 32)
                lanes = slice(128 * i, 128 * i + 128)
                for n, o in enumerate(fields):
                    hi, lo = split(t[64 * n : 64 * n + 32, lanes])
                    chi_ref[o, here, 0:128] = hi
                    clo_ref[o, here, 0:128] = lo
                    right_ref[o, before, 0:128] = hi
                    right_ref[o, before, 128:256] = lo
                    hi, lo = split(t[64 * n + 32 : 64 * n + 64, lanes])
                    chi_ref[o, here, 128:256] = hi
                    clo_ref[o, here, 128:256] = lo
                    left_ref[o, after, 0:128] = hi
                    left_ref[o, after, 128:256] = lo

    def streamwise(j, o, op, at):
        chi_ref, clo_ref, left_ref, right_ref = sets[j % 2]
        chi, clo = chi_ref[o], clo_ref[o]
        out = dot(chi, b_ref[op, 0]) + dot(clo, b_ref[op, 0]) + dot(chi, b_ref[op, 1])
        left, right = dot(left_ref[o], b_ref[op, 2]), dot(right_ref[o], b_ref[op, 3])
        first = out[:, 0:128] + (left[:, 0:128] + left[:, 128:256])
        second = out[:, 128:256] + (right[:, 0:128] + right[:, 128:256])
        for r in range(16):
            buf_ref[at, j, :, 256 * r : 256 * r + 128] = first[32 * r : 32 * r + 32]
            buf_ref[at, j, :, 256 * r + 128 : 256 * r + 256] = second[32 * r : 32 * r + 32]
        copy(at, j).start()

    for p in range(8):
        spanwise(0, p)
    for j in range(3):
        for step, (o, op, at) in enumerate(((0, 1, 0), (2, 0, 1), (1, 0, 2))):
            if j < 2:
                for p in ((0, 1, 2), (3, 4, 5), (6, 7))[step]:
                    spanwise(j + 1, p)
            streamwise(j, o, op, at)

    for o in range(3):
        for j in range(3):
            copy(o, j).wait()


def planes(received, zcat, blocks):
    vmem, hbm = pl.BlockSpec(memory_space=pltpu.VMEM), pl.BlockSpec(memory_space=pltpu.HBM)
    return pl.pallas_call(
        planes_kernel,
        out_shape=(jax.ShapeDtypeStruct((3, 32, 4096), F32),) * 3,
        in_specs=[vmem] * 3,
        out_specs=(hbm,) * 3,
        scratch_shapes=[pltpu.VMEM((3, 512, 256), BF16)] * 8
        + [pltpu.VMEM((3, 3, 32, 4096), F32), pltpu.SemaphoreType.DMA((3, 3))],
        compiler_params=params(32),
        cost_estimate=pl.CostEstimate(flops=4_000_000_000, bytes_accessed=8 << 20, transcendentals=0),
        name="planes",
    )(received.reshape(256 * 24, 128), zcat, blocks)


def per_device(velocity, stream_ops, normal_ops, span_ops):
    lines = lax.all_to_all(pack(velocity), "row", split_axis=0, concat_axis=0, tiled=True)
    fields, blocks, zcat = normal(lines, stream_ops, normal_ops, span_ops)
    fields = fields.reshape(256, 24, 128)
    fields = lax.all_to_all(fields, ("row", "col"), split_axis=0, concat_axis=0, tiled=True)
    grads = planes(fields, zcat, blocks)
    return tuple(g.transpose(1, 0, 2) for g in grads)


def solution(mesh):
    return jax.shard_map(
        per_device,
        mesh=mesh,
        in_specs=(P("col", "row", None), P(), P(), P()),
        out_specs=(P(None, ("row", "col"), None),) * 3,
        check_vma=False,
    )
```

```python
import jax
import jax.numpy as jnp
from jax import lax
from jax.experimental import pallas as pl
from jax.experimental.pallas import tpu as pltpu
from jax.sharding import PartitionSpec as P

F32 = jnp.float32
BF16 = jnp.bfloat16


def split(x):
    hi = x.astype(BF16)
    return hi, (x - hi.astype(F32)).astype(BF16)


def dot(a, b):
    return jnp.dot(a, b, preferred_element_type=F32)


def in_hbm(x):
    return pltpu.with_memory_space_constraint(x, pltpu.HBM)


def params(mib):
    return pltpu.CompilerParams(vmem_limit_bytes=mib << 20)


CHUNKS = 4


def pack_kernel(v_ref, o_ref, in_ref, sem):
    width, blocks = 4096 // CHUNKS, 16 // CHUNKS
    loads = [
        pltpu.make_async_copy(v_ref.at[:, :, pl.ds(width * i, width)], in_ref.at[i], sem.at[i])
        for i in range(CHUNKS)
    ]
    for load in loads:
        load.start()
    for i in range(CHUNKS):
        loads[i].wait()
        for d in range(blocks):
            for q in range(4):
                z, h = q // 2, q % 2
                lanes = slice(256 * d + 128 * h, 256 * d + 128 * h + 128)
                o_ref[blocks * i + d, 48 * q : 48 * q + 48, :] = in_ref[i, z, :, lanes]


def pack(velocity):
    return pl.pallas_call(
        pack_kernel,
        out_shape=jax.ShapeDtypeStruct((16, 192, 128), F32),
        in_specs=[pl.BlockSpec(memory_space=pltpu.HBM)],
        out_specs=pl.BlockSpec(memory_space=pltpu.VMEM),
        scratch_shapes=[
            pltpu.VMEM((CHUNKS, 2, 48, 4096 // CHUNKS), F32),
            pltpu.SemaphoreType.DMA((CHUNKS,)),
        ],
        compiler_params=params(8),
        cost_estimate=pl.CostEstimate(flops=0, bytes_accessed=3 << 20, transcendentals=0),
        name="pack",
    )(in_hbm(velocity))


def operators(s_ref, p_ref, b_ref, z_ref):
    zero = jnp.zeros((128, 128), BF16)
    for op in range(2):
        (lhi, llo), (ohi, olo), (rhi, rlo) = (split(s_ref[op, d].T) for d in range(3))
        tiles = (
            ((ohi, lhi), (rhi, ohi)),
            ((olo, llo), (rlo, olo)),
            ((lhi, llo), (lhi, zero)),
            ((rhi, rlo), (rhi, zero)),
        )
        for t, tile in enumerate(tiles):
            for k in range(2):
                for h in range(2):
                    b_ref[op, t, 128 * k : 128 * k + 128, 128 * h : 128 * h + 128] = tile[k][h]
    col = lax.broadcasted_iota(jnp.int32, (32, 256), 1)
    row = lax.broadcasted_iota(jnp.int32, (32, 256), 0)
    plane = 2 * (col % 16) + (col // 32) % 2
    for o, k in enumerate((0, 1, 0)):
        zhi, zlo = split(p_ref[k])
        for h in range(2):
            pick = jnp.where((plane == row) & ((col // 16) % 2 == h), 1.0, 0.0)
            first = jnp.where(col < 128, pick, 0.0).astype(BF16)
            last = jnp.where(col < 128, 0.0, pick).astype(BF16)
            at = 64 * o + 32 * h
            z_ref[at : at + 32, :] = (dot(zhi, first) + dot(zlo, last)).astype(BF16)


def normal_kernel(r_ref, n_ref, s_ref, p_ref, o_ref, b_ref, z_ref, vhi_ref, vlo_ref):
    for q in range(4):
        hi, lo = split(r_ref[:, 48 * q : 48 * q + 48, :].reshape(768, 128))
        vhi_ref[:, 128 * q : 128 * q + 128] = hi
        vlo_ref[:, 128 * q : 128 * q + 128] = lo

    def step(f, at):
        whi, wlo = split(n_ref[f, pl.ds(at, 256), :])
        vhi, vlo = vhi_ref[...], vlo_ref[...]
        out = dot(whi, vhi) + dot(whi, vlo) + dot(wlo, vhi)
        for q in range(4):
            o_ref[pl.ds(8 * at + 4 * f + q, 256, stride=8), :] = out[:, 128 * q : 128 * q + 128]

    for f in range(2):
        for t in range(3):
            step(f, 256 * t)
            if f == 0 and t == 0:
                operators(s_ref, p_ref, b_ref, z_ref)


def normal(received, stream_ops, normal_ops, span_ops):
    vmem = pl.BlockSpec(memory_space=pltpu.VMEM)
    return pl.pallas_call(
        normal_kernel,
        out_shape=(
            jax.ShapeDtypeStruct((256 * 24, 128), F32),
            jax.ShapeDtypeStruct((2, 4, 256, 256), BF16),
            jax.ShapeDtypeStruct((192, 256), BF16),
        ),
        in_specs=[vmem] * 4,
        out_specs=(vmem,) * 3,
        scratch_shapes=[pltpu.VMEM((768, 512), BF16), pltpu.VMEM((768, 512), BF16)],
        compiler_params=params(24),
        cost_estimate=pl.CostEstimate(flops=3_600_000_000, bytes_accessed=9 << 20, transcendentals=0),
        name="normal",
    )(received, normal_ops, stream_ops, span_ops)


def planes_kernel(r_ref, z_ref, b_ref, *refs):
    hbm, sets, (buf_ref, sem) = refs[:3], (refs[3:7], refs[7:11]), refs[11:]

    def copy(o, j):
        return pltpu.make_async_copy(buf_ref.at[o, j], hbm[o].at[j], sem.at[o, j])

    def spanwise(j, p):
        chi_ref, clo_ref, left_ref, right_ref = sets[j % 2]
        for f, rows, fields in ((0, slice(0, 128), (0, 1)), (1, slice(128, 192), (2,))):
            both = []
            for r in (2 * p, 2 * p + 1):
                lines = [r_ref[pl.ds(384 * r + 8 * j + 4 * f + q, 16, stride=24), :] for q in range(4)]
                both.append(jnp.concatenate(split(jnp.concatenate(lines, axis=0)) * 2, axis=0))
            t = dot(z_ref[rows, :], jnp.concatenate(both, axis=1))
            for i, r in enumerate((2 * p, 2 * p + 1)):
                here = slice(32 * r, 32 * r + 32)
                before = slice(32 * ((r - 1) % 16), 32 * ((r - 1) % 16) + 32)
                after = slice(32 * ((r + 1) % 16), 32 * ((r + 1) % 16) + 32)
                lanes = slice(128 * i, 128 * i + 128)
                for n, o in enumerate(fields):
                    hi, lo = split(t[64 * n : 64 * n + 32, lanes])
                    chi_ref[o, here, 0:128] = hi
                    clo_ref[o, here, 0:128] = lo
                    right_ref[o, before, 0:128] = hi
                    right_ref[o, before, 128:256] = lo
                    hi, lo = split(t[64 * n + 32 : 64 * n + 64, lanes])
                    chi_ref[o, here, 128:256] = hi
                    clo_ref[o, here, 128:256] = lo
                    left_ref[o, after, 0:128] = hi
                    left_ref[o, after, 128:256] = lo

    def streamwise(j, o, op, at):
        chi_ref, clo_ref, left_ref, right_ref = sets[j % 2]
        chi, clo = chi_ref[o], clo_ref[o]
        out = dot(chi, b_ref[op, 0]) + dot(clo, b_ref[op, 0]) + dot(chi, b_ref[op, 1])
        left, right = dot(left_ref[o], b_ref[op, 2]), dot(right_ref[o], b_ref[op, 3])
        first = out[:, 0:128] + (left[:, 0:128] + left[:, 128:256])
        second = out[:, 128:256] + (right[:, 0:128] + right[:, 128:256])
        for r in range(16):
            buf_ref[at, j, :, 256 * r : 256 * r + 128] = first[32 * r : 32 * r + 32]
            buf_ref[at, j, :, 256 * r + 128 : 256 * r + 256] = second[32 * r : 32 * r + 32]
        copy(at, j).start()

    for p in range(8):
        spanwise(0, p)
    for j in range(3):
        for step, (o, op, at) in enumerate(((0, 1, 0), (2, 0, 1), (1, 0, 2))):
            if j < 2:
                for p in ((0, 1, 2), (3, 4, 5), (6, 7))[step]:
                    spanwise(j + 1, p)
            streamwise(j, o, op, at)

    for o in range(3):
        for j in range(3):
            copy(o, j).wait()


def planes(received, zcat, blocks):
    vmem, hbm = pl.BlockSpec(memory_space=pltpu.VMEM), pl.BlockSpec(memory_space=pltpu.HBM)
    return pl.pallas_call(
        planes_kernel,
        out_shape=(jax.ShapeDtypeStruct((3, 32, 4096), F32),) * 3,
        in_specs=[vmem] * 3,
        out_specs=(hbm,) * 3,
        scratch_shapes=[pltpu.VMEM((3, 512, 256), BF16)] * 8
        + [pltpu.VMEM((3, 3, 32, 4096), F32), pltpu.SemaphoreType.DMA((3, 3))],
        compiler_params=params(32),
        cost_estimate=pl.CostEstimate(flops=4_000_000_000, bytes_accessed=8 << 20, transcendentals=0),
        name="planes",
    )(received.reshape(256 * 24, 128), zcat, blocks)


def per_device(velocity, stream_ops, normal_ops, span_ops):
    lines = lax.all_to_all(pack(velocity), "row", split_axis=0, concat_axis=0, tiled=True)
    fields, blocks, zcat = normal(lines, stream_ops, normal_ops, span_ops)
    fields = fields.reshape(256, 24, 128)
    fields = lax.all_to_all(fields, ("row", "col"), split_axis=0, concat_axis=0, tiled=True)
    grads = planes(fields, zcat, blocks)
    return tuple(g.transpose(1, 0, 2) for g in grads)


def solution(mesh):
    return jax.shard_map(
        per_device,
        mesh=mesh,
        in_specs=(P("col", "row", None), P(), P(), P()),
        out_specs=(P(None, ("row", "col"), None),) * 3,
        check_vma=False,
    )
```
